128 devices in a mesh: fsdp: 8 (over y_lo, z), ctx: 4 (over y_hi, core), tp: 4 (over x).
Axes of the slice: x: 4, y: 4 (y_hi: 2, y_lo: 2; y = y_hi * 2 + y_lo), z: 4, core: 2. Of those that a mesh axis runs over, the one named last changes fastest.
Arguments:
- inputs: bfloat16 [32, 1024, 960], P(('fsdp', 'tp'), 'ctx'), may hold values from -6 to 6
- seq_live: int32 [32], P(('fsdp', 'tp')), may hold values from 0 to 1, as said below
- positions: int32 [32, 1024], P(('fsdp', 'tp'), 'ctx'), may hold values from 0 to 2046, as said below
- gain_attn: bfloat16 [960], P('fsdp'), may hold values from 0.5 to 1.5
- w_query: bfloat16 [960, 960], P('fsdp'), may hold values from -0.75 to 0.75
- w_key: bfloat16 [960, 320], P('fsdp'), may hold values from -0.75 to 0.75
- w_value: bfloat16 [960, 320], P('fsdp'), may hold values from -0.1875 to 0.1875
- w_out: bfloat16 [960, 960], P('fsdp'), may hold values from -1.5 to 1.5
- gain_mlp: bfloat16 [960], P('fsdp'), may hold values from 0.5 to 1.5
- w_gate: bfloat16 [960, 2560], P('fsdp', 'tp'), may hold values from -0.1875 to 0.1875
- w_up: bfloat16 [960, 2560], P('fsdp', 'tp'), may hold values from -0.1875 to 0.1875
- w_down: bfloat16 [960, 2560], P('fsdp', 'tp'), may hold values from -0.125 to 0.125
- cotangent: float32 [32, 1024, 960], P(('fsdp', 'tp'), 'ctx'), may hold values from -6 to 6
Outputs:
- layer_out: float32 [32, 1024, 960], P(('fsdp', 'tp'), 'ctx')
- dinputs: float32 [32, 1024, 960], P(('fsdp', 'tp'), 'ctx')
- dgain_attn: float32 [960], P('fsdp')
- dw_query: float32 [960, 960], P('fsdp')
- dw_key: float32 [960, 320], P('fsdp')
- dw_value: float32 [960, 320], P('fsdp')
- dw_out: float32 [960, 960], P('fsdp')
- dgain_mlp: float32 [960], P('fsdp')
- dw_gate: float32 [960, 2560], P('fsdp', 'tp')
- dw_up: float32 [960, 2560], P('fsdp', 'tp')
- dw_down: float32 [960, 2560], P('fsdp', 'tp')
The draws below stay inside these ranges and needn't reach their ends.
Inputs may be any that keep to these rules, and one draw needn't show every extreme that they name: `seq_live`: the slots fall into equal blocks of consecutive slots, one block for each index of fsdp; each block holds either only 1s or exactly one 0, at any slot of the block, and both kinds of block occur. `positions`: each row starts at 0 and rises by 1 or 2 from token to token; the first slot's row rises by 2 throughout.
All inputs are finite; a program needn't handle non-finite values.
Results may differ from the reference program's by a relative error of at most 0.025.
Values may be sent and summed in bfloat16 or wider, within the bound.
No kernel may reach another device: no remote copies, remote signals or barrier semaphores. Data moves between devices by JAX's collectives and lax.ppermute only.
A program may use at most 128 MiB of HBM per device.

```python
import math
import jax
import jax.numpy as jnp
from jax import lax

D = 960
FF = 2560
QH = 15
KVH = 5
HEAD = 64
LEN = 1024
QD = 960
KVD = 320
SEQS = 32
N_FSDP = 8


def drawn_weight(key, width, salt):
    base = jax.random.normal(jax.random.fold_in(key, salt), (D, width), jnp.float32) * (1.0 / math.sqrt(D))
    return jnp.clip(base, -0.75, 0.75)


def draw_w_query(key, part):
    base = drawn_weight(key, QH * HEAD, 21)
    return base.astype(jnp.bfloat16)


def draw_w_key(key, part):
    base = drawn_weight(key, KVH * HEAD, 22)
    return base.astype(jnp.bfloat16)


def draw_inputs(key, part):
    values = jnp.clip(jax.random.normal(jax.random.fold_in(key, 23), (SEQS, LEN, D), jnp.float32), -6.0, 6.0)
    return values.astype(jnp.bfloat16)


def draw_seq_live(key, part):
    block_size = SEQS // N_FSDP
    short_flag = jax.random.randint(jax.random.fold_in(key, 31), (N_FSDP,), 0, 2, dtype=jnp.int32)
    order = jax.random.permutation(jax.random.fold_in(key, 32), N_FSDP)
    short_flag = short_flag.at[order[0]].set(0).at[order[1]].set(1)
    empty_slot = jax.random.randint(jax.random.fold_in(key, 33), (N_FSDP,), 0, block_size, dtype=jnp.int32)
    slot_index = jnp.arange(SEQS, dtype=jnp.int32) % block_size
    owner_index = jnp.arange(SEQS, dtype=jnp.int32) // block_size
    dead = (short_flag[owner_index] == 1) & (slot_index == empty_slot[owner_index])
    return jnp.where(dead, 0, 1).astype(jnp.int32)


def draw_positions(key, part):
    step_sizes = jax.random.randint(key, (SEQS, LEN), 1, 3, dtype=jnp.int32)
    step_sizes = step_sizes.at[0].set(2)
    running = jnp.cumsum(step_sizes, axis=1)
    return (running - step_sizes[:, :1]).astype(jnp.int32)


def shard_levels(rng, dims, shards, smallest, top_value):
    def one(axis_at, parts):
        heights = jax.random.uniform(jax.random.fold_in(jax.random.fold_in(rng, 6), axis_at), (parts,), jnp.float32, smallest / len(shards), top_value / len(shards))
        return jnp.repeat(jnp.exp(heights), dims[axis_at] // parts).reshape((-1,) + (1,) * (len(dims) - axis_at - 1))

    factor_of = one(*shards[0])
    for cut in shards[1:]:
        factor_of = factor_of * one(*cut)
    return factor_of


def normal_values(rng, shape, deviation, most, cuts=(), kind=jnp.bfloat16):
    array = jax.random.normal(rng, shape, jnp.float32) * deviation
    if len(cuts) > 0:
        array = shard_levels(rng, shape, cuts, -0.22, 0.18) * array
    return jnp.clip(array, min=-most, max=most).astype(kind)


def setup_inputs(seed: int = 0) -> dict:
    seeds = jax.random.split(jax.random.key(seed), 14)
    return {
        "inputs": draw_inputs(jax.random.fold_in(seeds[13], 71), 0),
        "seq_live": draw_seq_live(jax.random.fold_in(seeds[13], 71), 0),
        "positions": draw_positions(jax.random.fold_in(seeds[13], 71), 0),
        "gain_attn": jnp.clip(1.0 + 0.1 * jax.random.normal(seeds[3], (D,), jnp.float32), 0.5, 1.5).astype(jnp.bfloat16),
        "w_query": draw_w_query(jax.random.fold_in(seeds[13], 71), 0),
        "w_key": draw_w_key(jax.random.fold_in(seeds[13], 71), 0),
        "w_value": normal_values(seeds[6], (D, KVD), D ** -0.5, 0.1875, ((0, 8),)),
        "w_out": normal_values(seeds[7], (QD, D), (max(QH * HEAD * 16 // LEN, 1)) ** -0.5, 1.5, ((0, 8),)),
        "gain_mlp": jnp.clip(1.0 + 0.1 * jax.random.normal(seeds[8], (D,), jnp.float32), 0.5, 1.5).astype(jnp.bfloat16),
        "w_gate": normal_values(seeds[9], (D, FF), D ** -0.5, 0.1875, ((0, 8), (1, 4))),
        "w_up": normal_values(seeds[10], (D, FF), D ** -0.5, 0.1875, ((0, 8), (1, 4))),
        "w_down": normal_values(seeds[11], (D, FF), FF ** -0.5, 0.125, ((0, 8), (1, 4))),
        "cotangent": normal_values(seeds[12], (SEQS, LEN, D), 1.0, 6.0, ((0, 32), (1, 4)), jnp.float32),
    }


EPSILON = 1e-05
ROPE_BASE = 100000.0

def rope_tables(position_ids):
    half_dim = HEAD // 2
    freq_index = jnp.arange(half_dim, dtype=jnp.float32)
    inverse = jnp.exp(freq_index * (-2.0 * math.log(ROPE_BASE) / HEAD))
    angles = position_ids.astype(jnp.float32)[:, None] * inverse[None, :]
    return (jnp.cos(angles)[:, None, :], jnp.sin(angles)[:, None, :])

def rotate(tensor, cos_table, sin_table):
    half_dim = tensor.shape[-1] // 2
    first_half = tensor[..., :half_dim]
    second_half = tensor[..., half_dim:]
    return jnp.concatenate([first_half * cos_table - second_half * sin_table, second_half * cos_table + first_half * sin_table], -1)

def rotate_back(tensor, cos_table, sin_table):
    half_dim = tensor.shape[-1] // 2
    first_half = tensor[..., :half_dim]
    second_half = tensor[..., half_dim:]
    return jnp.concatenate([first_half * cos_table + second_half * sin_table, second_half * cos_table - first_half * sin_table], -1)

def rms_forward(stream, gain_vector):
    scale_inv = lax.rsqrt(lax.optimization_barrier(jnp.mean(stream * stream, -1, keepdims=True)) + EPSILON)
    normed = stream * scale_inv
    return (scale_inv, normed, (normed * gain_vector.astype(jnp.float32)).astype(jnp.bfloat16))

def rms_backward(upstream, scale_inv, normed, gain_vector):
    scaled = upstream * gain_vector.astype(jnp.float32)
    inner_mean = lax.optimization_barrier(jnp.mean(scaled * normed, -1, keepdims=True))
    return (scale_inv * (scaled - normed * inner_mean), lax.optimization_barrier(jnp.sum(upstream * normed, 0)))

def reference(inputs, seq_live, positions, gain_attn, w_query, w_key, w_value, w_out, gain_mlp, w_gate, w_up, w_down, cotangent):
    group_size = QH // KVH
    score_scale = 1.0 / math.sqrt(HEAD)
    contract_rows = (((0,), (0,)), ((), ()))
    contract_cols = (((1,), (1,)), ((), ()))
    allowed = jnp.arange(LEN)[:, None] >= jnp.arange(LEN)[None, :]

    def one_sequence(totals, pieces):
        seq_input, seq_pos, live_flag, seq_cot = pieces
        stream = seq_input.astype(jnp.float32)
        inv_one, normed_one, hidden_one = rms_forward(stream, gain_attn)
        cos_table, sin_table = rope_tables(seq_pos)
        query_lin = jnp.dot(hidden_one, w_query, preferred_element_type=jnp.float32).reshape(LEN, QH, HEAD)
        queries = rotate(query_lin, cos_table, sin_table).astype(jnp.bfloat16)
        key_lin = jnp.dot(hidden_one, w_key, preferred_element_type=jnp.float32).reshape(LEN, KVH, HEAD)
        key_rows = rotate(key_lin, cos_table, sin_table).astype(jnp.bfloat16)
        value_rows = jnp.dot(hidden_one, w_value, preferred_element_type=jnp.float32).astype(jnp.bfloat16).reshape(LEN, KVH, HEAD)
        query_groups = queries.reshape(LEN, KVH, group_size, HEAD).astype(jnp.float32)
        key_float = key_rows.astype(jnp.float32)
        value_float = value_rows.astype(jnp.float32)
        scores = jnp.einsum('qhgd,khd->hgqk', query_groups, key_float) * score_scale
        scores = jnp.where(allowed, scores, -1e+30)
        row_top = lax.optimization_barrier(jnp.max(scores, -1, keepdims=True))
        log_total = row_top + jnp.log(lax.optimization_barrier(jnp.sum(jnp.exp(scores - row_top), -1, keepdims=True)))
        softmax = jnp.exp(scores - log_total)
        probs_b = softmax.astype(jnp.bfloat16).astype(jnp.float32)
        attended = jnp.einsum('hgqk,khd->qhgd', probs_b, value_float).astype(jnp.bfloat16).reshape(LEN, QH * HEAD)
        mid_stream = stream + jnp.dot(attended, w_out, preferred_element_type=jnp.float32)
        inv_two, normed_two, hidden_two = rms_forward(mid_stream, gain_mlp)
        gate_pre = jnp.dot(hidden_two, w_gate, preferred_element_type=jnp.float32)
        up_pre = jnp.dot(hidden_two, w_up, preferred_element_type=jnp.float32)
        sigmoid_gate = jax.nn.sigmoid(gate_pre)
        activated = (gate_pre * sigmoid_gate * up_pre).astype(jnp.bfloat16)
        layer_out = mid_stream + lax.dot_general(activated, w_down, contract_cols, preferred_element_type=jnp.float32)
        upstream = seq_cot * live_flag.astype(jnp.float32)
        upstream_b = upstream.astype(jnp.bfloat16)
        grad_act = jnp.dot(upstream_b, w_down, preferred_element_type=jnp.float32)
        up_back = (grad_act * gate_pre * sigmoid_gate).astype(jnp.bfloat16)
        gate_back = (grad_act * up_pre * sigmoid_gate * (1.0 + gate_pre * (1.0 - sigmoid_gate))).astype(jnp.bfloat16)
        down_term = lax.dot_general(upstream_b, activated, contract_rows, preferred_element_type=jnp.float32)
        gate_term = lax.dot_general(hidden_two, gate_back, contract_rows, preferred_element_type=jnp.float32)
        up_term = lax.dot_general(hidden_two, up_back, contract_rows, preferred_element_type=jnp.float32)
        grad_hidden_two = lax.dot_general(gate_back, w_gate, contract_cols, preferred_element_type=jnp.float32) + lax.dot_general(up_back, w_up, contract_cols, preferred_element_type=jnp.float32)
        back_two, gain_two_term = rms_backward(grad_hidden_two, inv_two, normed_two, gain_mlp)
        grad_mid = upstream + back_two
        grad_mid_b = grad_mid.astype(jnp.bfloat16)
        out_term = lax.dot_general(attended, grad_mid_b, contract_rows, preferred_element_type=jnp.float32)
        grad_attended = lax.dot_general(grad_mid_b, w_out, contract_cols, preferred_element_type=jnp.float32).astype(jnp.bfloat16)
        grad_attended = grad_attended.reshape(LEN, KVH, group_size, HEAD).astype(jnp.float32)
        grad_probs = jnp.einsum('qhgd,khd->hgqk', grad_attended, value_float)
        row_inner = lax.optimization_barrier(jnp.sum(softmax * grad_probs, -1, keepdims=True))
        grad_scores = (softmax * (grad_probs - row_inner) * score_scale).astype(jnp.bfloat16).astype(jnp.float32)
        grad_values = jnp.einsum('hgqk,qhgd->khd', probs_b, grad_attended)
        grad_keys = jnp.einsum('hgqk,qhgd->khd', grad_scores, query_groups)
        grad_queries = jnp.einsum('hgqk,khd->qhgd', grad_scores, key_float).reshape(LEN, QH, HEAD)
        grad_query_lin = rotate_back(grad_queries, cos_table, sin_table).astype(jnp.bfloat16).reshape(LEN, QH * HEAD)
        grad_key_lin = rotate_back(grad_keys, cos_table, sin_table).astype(jnp.bfloat16).reshape(LEN, KVH * HEAD)
        grad_value_lin = grad_values.astype(jnp.bfloat16).reshape(LEN, KVH * HEAD)
        query_term = lax.dot_general(hidden_one, grad_query_lin, contract_rows, preferred_element_type=jnp.float32)
        key_term = lax.dot_general(hidden_one, grad_key_lin, contract_rows, preferred_element_type=jnp.float32)
        value_term = lax.dot_general(hidden_one, grad_value_lin, contract_rows, preferred_element_type=jnp.float32)
        grad_hidden_one = lax.dot_general(grad_query_lin, w_query, contract_cols, preferred_element_type=jnp.float32)
        grad_hidden_one = grad_hidden_one + lax.dot_general(grad_key_lin, w_key, contract_cols, preferred_element_type=jnp.float32)
        grad_hidden_one = grad_hidden_one + lax.dot_general(grad_value_lin, w_value, contract_cols, preferred_element_type=jnp.float32)
        back_one, gain_one_term = rms_backward(grad_hidden_one, inv_one, normed_one, gain_attn)
        grad_input = grad_mid + back_one
        terms = (gain_one_term, query_term, key_term, value_term, out_term, gain_two_term, gate_term, up_term, down_term)
        new_totals = tuple((total_part + term_part for total_part, term_part in zip(totals, terms)))
        return (new_totals, (layer_out, grad_input))
    init = (jnp.zeros((D,), jnp.float32), jnp.zeros((D, QH * HEAD), jnp.float32), jnp.zeros((D, KVH * HEAD), jnp.float32), jnp.zeros((D, KVH * HEAD), jnp.float32), jnp.zeros((QH * HEAD, D), jnp.float32), jnp.zeros((D,), jnp.float32), jnp.zeros((D, FF), jnp.float32), jnp.zeros((D, FF), jnp.float32), jnp.zeros((D, FF), jnp.float32))
    totals, results = lax.scan(one_sequence, init, (inputs, positions, seq_live, cotangent))
    return (results[0], results[1], totals[0], totals[1], totals[2], totals[3], totals[4], totals[5], totals[6], totals[7], totals[8])
```

```python
import math

import jax
import jax.numpy as jnp
from jax import lax
from jax.experimental import pallas as pl
from jax.experimental.pallas import tpu as pltpu
from jax.sharding import PartitionSpec as P

QH = 15
KVH = 5
HEAD = 64
GROUP = QH // KVH
EPSILON = 1e-05
ROPE_BASE = 100000.0
SCALE = 1.0 / math.sqrt(HEAD)
NEG = -1e30
BF = jnp.bfloat16
F32 = jnp.float32

HALF_A = 832
HALF_B = 768
HALF_W = 896
FF_HALF = 320
FF_PAD = 384
OUT_HALF = 480
OUT_PAD = 512

CORE_SWAP = [(i, i ^ 1) for i in range(4)]
ROW_SWAP = [(i, i ^ 2) for i in range(4)]
ROW_UP = [(0, 2), (1, 3)]
ROW_DOWN = [(2, 0), (3, 1)]


def dot(a, b, ca, cb):
    return lax.dot_general(a, b, (((ca,), (cb,)), ((), ())), preferred_element_type=F32)


def after(value, *others):
    return lax.optimization_barrier((value, *others))[0]


def from_fsdp(shard):
    copies = jnp.broadcast_to(shard, (lax.axis_size("fsdp"), *shard.shape))
    out = lax.all_to_all(copies, "fsdp", split_axis=0, concat_axis=0, tiled=True)
    return out.reshape(-1, shard.shape[1])


def to_fsdp(full):
    n = lax.axis_size("fsdp")
    tiles = full.reshape(n, full.shape[0] // n, full.shape[1])
    out = lax.all_to_all(tiles, "fsdp", split_axis=0, concat_axis=0, tiled=True)
    return out.astype(F32).sum(axis=0)


def shift(x, by):
    return lax.ppermute(x, "tp", [(i, (i + by) % 4) for i in range(4)])


def tp_blocks(x):
    return [x, shift(x, 1), shift(x, 3), shift(x, 2)]


def tp_sum(own, left, right, far):
    a, b, c = shift(left, 3), shift(right, 1), shift(far, 2)
    return own + a.astype(F32) + b.astype(F32) + c.astype(F32)


def swap_core(x):
    return lax.ppermute(x, "ctx", CORE_SWAP)


def rms_forward(stream, gain_row):
    scale_inv = lax.rsqrt(jnp.mean(stream * stream, -1, keepdims=True) + EPSILON)
    normed = stream * scale_inv
    return scale_inv, normed, (normed * gain_row).astype(BF)


def rms_backward(upstream, scale_inv, normed, gain_row):
    scaled = upstream * gain_row
    inner_mean = jnp.mean(scaled * normed, -1, keepdims=True)
    return scale_inv * (scaled - normed * inner_mean), jnp.sum(upstream * normed, 0)


def turned(x, c, s):
    u1, u2 = x[:32], x[32:]
    return jnp.concatenate([u1 * c - u2 * s, u2 * c + u1 * s], 0)


def turned_back(x, c, s):
    u1, u2 = x[:32], x[32:]
    return jnp.concatenate([u1 * c + u2 * s, u2 * c - u1 * s], 0)


def score_block(keys, queries, b, bias_ref, tri):
    s = dot(keys[b * 256 : (b + 1) * 256], queries, 1, 0) * SCALE
    if b == 0:
        return jnp.where(tri, s, NEG)
    return s + bias_ref[0 if b == 1 else 1]


def triangle():
    u = lax.broadcasted_iota(jnp.int32, (256, 256), 0)
    t = lax.broadcasted_iota(jnp.int32, (256, 256), 1)
    return u <= t


def attend_body(bias, q, k, v, cos, sin, q_out, k_out, att, lse):
    c, s = cos[...], sin[...]
    kb = turned(k[...], c, s).astype(BF)
    k_out[...] = kb
    keys = kb.T
    tri = triangle()
    for g in range(GROUP):
        rows = slice(g * HEAD, (g + 1) * HEAD)
        qb = turned(q[rows, :], c[:, :256], s[:, :256]).astype(BF)
        q_out[rows, :] = qb
        parts = [score_block(keys, qb, b, bias, tri) for b in range(4)]
        tops = [jnp.max(p, 0, keepdims=True) for p in parts]
        top = jnp.maximum(jnp.maximum(tops[0], tops[1]), jnp.maximum(tops[2], tops[3]))
        total = jnp.zeros_like(top)
        out = jnp.zeros((HEAD, 256), F32)
        for b in range(4):
            p = jnp.exp(parts[b] - top)
            total = total + jnp.sum(p, 0, keepdims=True)
            out = out + dot(v[:, b * 256 : (b + 1) * 256], p.astype(BF), 1, 0)
        att[rows, :] = (out / total).astype(BF)
        lse[0, g : g + 1, :] = top + jnp.log(total)
    lse[0, GROUP:, :] = jnp.zeros((8 - GROUP, 256), F32)


def attend_back_body(bias, q, k, v, d, lse, cos, sin, dq, dk, dv):
    c, s = cos[...], sin[...]
    keys, values = k[...].T, v[...].T
    tri = triangle()
    dk_sum = [jnp.zeros((HEAD, 256), F32) for _ in range(4)]
    dv_sum = [jnp.zeros((HEAD, 256), F32) for _ in range(4)]
    for g in range(GROUP):
        rows = slice(g * HEAD, (g + 1) * HEAD)
        qb, db = q[rows, :], d[rows, :]
        log_total = lse[0, g : g + 1, :]
        probs, grads = [], []
        inner = jnp.zeros((1, 256), F32)
        for b in range(4):
            p = jnp.exp(score_block(keys, qb, b, bias, tri) - log_total)
            gp = dot(values[b * 256 : (b + 1) * 256], db, 1, 0)
            inner = inner + jnp.sum(p * gp, 0, keepdims=True)
            probs.append(p)
            grads.append(gp)
        dq_sum = jnp.zeros((HEAD, 256), F32)
        for b in range(4):
            ds = (probs[b] * (grads[b] - inner) * SCALE).astype(BF)
            dv_sum[b] = dv_sum[b] + dot(db, probs[b].astype(BF), 1, 1)
            dk_sum[b] = dk_sum[b] + dot(qb, ds, 1, 1)
            dq_sum = dq_sum + dot(k[:, b * 256 : (b + 1) * 256], ds, 1, 0)
        dq[rows, :] = turned_back(dq_sum, c[:, :256], s[:, :256]).astype(BF)
    for b in range(4):
        cols = slice(b * 256, (b + 1) * 256)
        dk[:, cols] = turned_back(dk_sum[b], c[:, cols], s[:, cols]).astype(BF)
        dv[:, cols] = dv_sum[b].astype(BF)


def per_head(rows, cols):
    return pl.BlockSpec((rows, cols), lambda j: (j, 0))


def whole(rows, cols):
    return pl.BlockSpec((rows, cols), lambda j: (0, 0))


LSE_SPEC = pl.BlockSpec((1, 8, 256), lambda j: (j, 0, 0))
SMEM_SPEC = pl.BlockSpec(memory_space=pltpu.SMEM)


def attend(bias, q, k, v, cos, sin):
    gr = GROUP * HEAD
    return pl.pallas_call(
        attend_body,
        grid=(KVH,),
        in_specs=[SMEM_SPEC, per_head(gr, 256), per_head(HEAD, 1024), per_head(HEAD, 1024), whole(32, 1024), whole(32, 1024)],
        out_specs=[per_head(gr, 256), per_head(HEAD, 1024), per_head(gr, 256), LSE_SPEC],
        out_shape=[
            jax.ShapeDtypeStruct((QH * HEAD, 256), BF),
            jax.ShapeDtypeStruct((KVH * HEAD, 1024), BF),
            jax.ShapeDtypeStruct((QH * HEAD, 256), BF),
            jax.ShapeDtypeStruct((KVH, 8, 256), F32),
        ],
        name="attend",
    )(bias, q, k, v, cos, sin)


def attend_back(bias, q, k, v, d, lse, cos, sin):
    gr = GROUP * HEAD
    return pl.pallas_call(
        attend_back_body,
        grid=(KVH,),
        in_specs=[
            SMEM_SPEC,
            per_head(gr, 256),
            per_head(HEAD, 1024),
            per_head(HEAD, 1024),
            per_head(gr, 256),
            LSE_SPEC,
            whole(32, 1024),
            whole(32, 1024),
        ],
        out_specs=[per_head(gr, 256), per_head(HEAD, 1024), per_head(HEAD, 1024)],
        out_shape=[
            jax.ShapeDtypeStruct((QH * HEAD, 256), BF),
            jax.ShapeDtypeStruct((KVH * HEAD, 1024), BF),
            jax.ShapeDtypeStruct((KVH * HEAD, 1024), BF),
        ],
        name="attend_back",
    )(bias, q, k, v, d, lse, cos, sin)


def shards(
    inputs,
    seq_live,
    positions,
    gain_attn,
    w_query,
    w_key,
    w_value,
    w_out,
    gain_mlp,
    w_gate,
    w_up,
    w_down,
    cotangent,
):
    ctx = lax.axis_index("ctx")
    core = ctx & 1
    first = core == 0
    bias = jnp.where(jnp.stack([core == 1, ctx >= 2]), 0.0, NEG).astype(F32)
    x = inputs[0]
    rows, width = x.shape
    part = w_query.shape[0]

    gains = jnp.pad(jnp.stack([gain_attn, gain_mlp], 1), ((0, 0), (0, HALF_W - HALF_A - 2)))
    half_a = jnp.concatenate([w_query[:, :HALF_A], gains], 1)
    half_b = jnp.concatenate(
        [w_query[:, HALF_A:], w_key, w_value, jnp.zeros((part, HALF_A - HALF_B), BF), gains], 1
    )
    qkv_mine = from_fsdp(jnp.where(first, half_a, half_b))
    qkv_theirs = swap_core(qkv_mine)

    upstream = cotangent[0] * seq_live.astype(F32)[:, None]
    grad_rows = jnp.concatenate(tp_blocks(upstream.astype(BF)), 0)

    earlier = lax.ppermute(x, "ctx", ROW_UP)
    earlier_pos = lax.ppermute(positions, "ctx", ROW_UP)
    beside = swap_core(jnp.stack([x, earlier]))
    beside_pos = swap_core(jnp.concatenate([positions, earlier_pos], 0))
    tokens = jnp.concatenate([x, beside[0], earlier, beside[1]], 0)
    all_pos = jnp.concatenate([positions, beside_pos[:1], earlier_pos, beside_pos[1:]], 1)

    out_part = jnp.where(first, w_out[:, :OUT_HALF], w_out[:, OUT_HALF:])
    out_mine = from_fsdp(after(jnp.pad(out_part, ((0, 0), (0, OUT_PAD - OUT_HALF))), qkv_mine))
    out_theirs = swap_core(out_mine)

    def ff_half(w):
        return jnp.pad(
            jnp.where(first, w[:, :FF_HALF], w[:, FF_HALF:]), ((0, 0), (0, FF_PAD - FF_HALF))
        )

    ff_part = jnp.concatenate([ff_half(w_gate), ff_half(w_up), ff_half(w_down)], 1)
    ff_mine = from_fsdp(after(ff_part, out_mine))
    ff_theirs = swap_core(ff_mine)
    full_gate, full_up, full_down = (
        jnp.concatenate(
            [ff_mine[:, i * FF_PAD : (i + 1) * FF_PAD], ff_theirs[:, i * FF_PAD : (i + 1) * FF_PAD]],
            1,
        )
        for i in range(3)
    )

    inverse = jnp.exp(jnp.arange(32, dtype=F32) * (-2.0 * math.log(ROPE_BASE) / HEAD))
    angles = inverse[:, None] * all_pos.astype(F32)
    cos, sin = jnp.cos(angles), jnp.sin(angles)
    gain_rows = qkv_mine[:, HALF_A : HALF_A + 2].astype(F32).T
    gain_one, gain_two = gain_rows[:1], gain_rows[1:]
    full_a = jnp.where(first, qkv_mine, qkv_theirs)[:, :HALF_A]
    full_b = jnp.where(first, qkv_theirs, qkv_mine)[:, :HALF_B]
    _, _, hidden_all = rms_forward(tokens.astype(F32), gain_one)
    stream = x.astype(F32)
    inv_one, normed_one, hidden_one = rms_forward(stream, gain_one)
    q_lin = jnp.concatenate(
        [dot(full_a, hidden_one, 0, 1), dot(full_b[:, :128], hidden_one, 0, 1)], 0
    )
    k_lin = dot(full_b[:, 128:448], hidden_all, 0, 1)
    values = dot(full_b[:, 448:768], hidden_all, 0, 1).astype(BF)
    queries, keys, attended, lse = attend(bias, q_lin, k_lin, values, cos, sin)

    full_out = jnp.concatenate(
        [
            jnp.where(first, out_mine, out_theirs)[:, :OUT_HALF],
            jnp.where(first, out_theirs, out_mine)[:, :OUT_HALF],
        ],
        1,
    )
    mid = stream + dot(attended, full_out, 0, 0)
    inv_two, normed_two, hidden_two = rms_forward(mid, gain_two)

    mlp_in = jnp.concatenate(tp_blocks(hidden_two), 0)
    gate_pre = dot(mlp_in, full_gate, 1, 0)
    up_pre = dot(mlp_in, full_up, 1, 0)
    sg = jax.nn.sigmoid(gate_pre)
    grad_act = dot(grad_rows, full_down, 1, 0)
    up_back = (grad_act * gate_pre * sg).astype(BF)
    gate_back = (grad_act * up_pre * sg * (1.0 + gate_pre * (1.0 - sg))).astype(BF)
    activated = (gate_pre * sg * up_pre).astype(BF)
    partial_in = dot(gate_back, full_gate, 1, 1) + dot(up_back, full_up, 1, 1)
    partial_in = partial_in.reshape(4, rows, width)
    grad_hidden_two = tp_sum(partial_in[0], *(partial_in[i].astype(BF) for i in (1, 2, 3)))

    partial_out = dot(activated, full_down, 1, 1).reshape(4, rows, width)
    layer_out = mid + tp_sum(partial_out[0], *(partial_out[i].astype(BF) for i in (1, 2, 3)))

    dw_ff = [
        dot(mlp_in, gate_back, 0, 0).astype(BF),
        dot(mlp_in, up_back, 0, 0).astype(BF),
        dot(grad_rows, activated, 0, 0).astype(BF),
    ]
    ff_sent = swap_core(jnp.concatenate([w[:, FF_PAD:] for w in dw_ff], 1))
    ff_kept = jnp.concatenate([w[:, :FF_PAD] for w in dw_ff], 1)
    ff_pair = (ff_kept.astype(F32) + ff_sent.astype(F32)).astype(BF)
    ff_sum = to_fsdp(ff_pair).astype(BF)

    back_two, dgain_two = rms_backward(grad_hidden_two, inv_two, normed_two, gain_two)
    grad_mid = upstream + back_two
    grad_mid_b = grad_mid.astype(BF)
    grad_attended = dot(full_out, grad_mid_b, 1, 1).astype(BF)
    dq, dk, dv = attend_back(bias, queries, keys, values, grad_attended, lse, cos, sin)

    dw_out = dot(attended, grad_mid_b, 1, 0).astype(BF)
    pad_out = ((0, 0), (0, OUT_PAD - OUT_HALF))
    out_l = jnp.pad(dw_out[:, :OUT_HALF], pad_out)
    out_r = jnp.pad(dw_out[:, OUT_HALF:], pad_out)
    out_sent = swap_core(jnp.where(first, out_r, out_l))
    out_pair = (jnp.where(first, out_l, out_r).astype(F32) + out_sent.astype(F32)).astype(BF)
    out_sum = to_fsdp(after(out_pair, ff_sum)).astype(BF)

    dkv = jnp.concatenate([dk, dv], 0)
    from_beside = swap_core(jnp.concatenate([dkv[:, 256:512], dkv[:, 768:1024]], 1))
    own_pair = dkv[:, :256].astype(F32) + from_beside[:, :256].astype(F32)
    earlier_pair = dkv[:, 512:768].astype(F32) + from_beside[:, 256:].astype(F32)
    from_later = lax.ppermute(earlier_pair.astype(BF), "ctx", ROW_DOWN)
    own_kv = (own_pair + from_later.astype(F32)).astype(BF)
    grad_hidden_one = (
        dot(dq[:HALF_A], full_a, 0, 1)
        + dot(dq[HALF_A:], full_b[:, :128], 0, 1)
        + dot(own_kv, full_b[:, 128:], 0, 1)
    )
    back_one, dgain_one = rms_backward(grad_hidden_one, inv_one, normed_one, gain_one)
    grad_input = grad_mid + back_one

    dgains = jnp.pad(
        jnp.stack([dgain_one, dgain_two], 0).T.astype(BF), ((0, 0), (0, HALF_W - HALF_A - 2))
    )
    grad_a = jnp.concatenate([dot(hidden_one, dq[:HALF_A], 0, 1).astype(BF), dgains], 1)
    grad_b = jnp.concatenate(
        [
            dot(hidden_one, dq[HALF_A:], 0, 1).astype(BF),
            dot(hidden_all, dk, 0, 1).astype(BF),
            dot(hidden_all, dv, 0, 1).astype(BF),
            jnp.zeros((width, HALF_A - HALF_B), BF),
            dgains,
        ],
        1,
    )
    qkv_sent = swap_core(jnp.where(first, grad_b, grad_a))
    qkv_pair = (jnp.where(first, grad_a, grad_b).astype(F32) + qkv_sent.astype(F32)).astype(BF)
    qkv_sum = to_fsdp(after(qkv_pair, out_sum)).astype(BF)

    def both_rows(v):
        return v.astype(F32) + lax.ppermute(v, "ctx", ROW_SWAP).astype(F32)

    def all_tp(v):
        for pairs in ([(0, 1), (1, 0), (2, 3), (3, 2)], [(0, 3), (3, 0), (1, 2), (2, 1)]):
            v = (v.astype(F32) + lax.ppermute(v, "tp", pairs).astype(F32)).astype(BF)
        return v

    ff_own = both_rows(ff_sum)
    ff_other = swap_core(ff_own)
    ff_lo, ff_hi = jnp.where(first, ff_own, ff_other), jnp.where(first, ff_other, ff_own)
    dw_gate, dw_up, dw_down = (
        jnp.concatenate([v[:, i * FF_PAD : i * FF_PAD + FF_HALF] for v in (ff_lo, ff_hi)], 1)
        for i in range(3)
    )
    out_own = both_rows(all_tp(out_sum))
    out_other = swap_core(out_own)
    out_lo, out_hi = jnp.where(first, out_own, out_other), jnp.where(first, out_other, out_own)
    dw_out = jnp.concatenate([out_lo[:, :OUT_HALF], out_hi[:, :OUT_HALF]], 1)
    qkv_own = both_rows(all_tp(qkv_sum))
    qkv_other = swap_core(qkv_own)
    got_a, got_b = jnp.where(first, qkv_own, qkv_other), jnp.where(first, qkv_other, qkv_own)
    return (
        layer_out[None],
        grad_input[None],
        got_a[:, HALF_A],
        jnp.concatenate([got_a[:, :HALF_A], got_b[:, :128]], 1),
        got_b[:, 128:448],
        got_b[:, 448:768],
        dw_out,
        got_a[:, HALF_A + 1],
        dw_gate,
        dw_up,
        dw_down,
    )


def solution(mesh):
    seqs, tokens = P(("fsdp", "tp"), "ctx", None), P(("fsdp", "tp"), "ctx")
    row, both = P("fsdp", None), P("fsdp", "tp")
    return jax.shard_map(
        shards,
        mesh=mesh,
        in_specs=(seqs, P(("fsdp", "tp")), tokens, P("fsdp"), row, row, row, row, P("fsdp"), both, both, both, seqs),
        out_specs=(seqs, seqs, P("fsdp"), row, row, row, row, P("fsdp"), both, both, both),
        check_vma=False,
    )
```

```python
import math

import jax
import jax.numpy as jnp
from jax import lax
from jax.experimental import pallas as pl
from jax.experimental.pallas import tpu as pltpu
from jax.sharding import PartitionSpec as P

QH = 15
KVH = 5
HEAD = 64
GROUP = QH // KVH
EPSILON = 1e-05
ROPE_BASE = 100000.0
SCALE = 1.0 / math.sqrt(HEAD)
NEG = -1e30
BF = jnp.bfloat16
F32 = jnp.float32

Q_A = 768
Q_B = 192
KV = 640
GAIN_AT = 832
HALF_W = 896
FF_HALF = 320
FF_PAD = 384
OUT_HALF = 480
OUT_PAD = 512

CORE_SWAP = [(i, i ^ 1) for i in range(4)]
ROW_SWAP = [(i, i ^ 2) for i in range(4)]
ROW_UP = [(0, 2), (1, 3)]
ROW_DOWN = [(2, 0), (3, 1)]


def dot(a, b, ca, cb):
    return lax.dot_general(a, b, (((ca,), (cb,)), ((), ())), preferred_element_type=F32)


def after(value, *others):
    return lax.optimization_barrier((value, *others))[0]


def from_fsdp(shard):
    copies = jnp.broadcast_to(shard, (lax.axis_size("fsdp"), *shard.shape))
    out = lax.all_to_all(copies, "fsdp", split_axis=0, concat_axis=0, tiled=True)
    return out.reshape(-1, shard.shape[1])


def to_fsdp(full):
    n = lax.axis_size("fsdp")
    tiles = full.reshape(n, full.shape[0] // n, full.shape[1])
    return lax.all_to_all(tiles, "fsdp", split_axis=0, concat_axis=0, tiled=True)


def summed(arrived):
    return arrived.astype(F32).sum(axis=0).astype(BF)


def shift(x, by):
    return lax.ppermute(x, "tp", [(i, (i + by) % 4) for i in range(4)])


def tp_blocks(x):
    return [x, shift(x, 1), shift(x, 3), shift(x, 2)]


def tp_sum(own, left, right, far):
    a, b, c = shift(left, 3), shift(right, 1), shift(far, 2)
    return own + a.astype(F32) + b.astype(F32) + c.astype(F32)


def swap_core(x):
    return lax.ppermute(x, "ctx", CORE_SWAP)


def rms_forward(stream, gain_row):
    scale_inv = lax.rsqrt(jnp.mean(stream * stream, -1, keepdims=True) + EPSILON)
    normed = stream * scale_inv
    return scale_inv, normed, (normed * gain_row).astype(BF)


def rms_backward(upstream, scale_inv, normed, gain_row):
    scaled = upstream * gain_row
    inner_mean = jnp.mean(scaled * normed, -1, keepdims=True)
    return scale_inv * (scaled - normed * inner_mean), jnp.sum(upstream * normed, 0)


def turned(x, c, s):
    u1, u2 = x[:32], x[32:]
    return jnp.concatenate([u1 * c - u2 * s, u2 * c + u1 * s], 0)


def turned_back(x, c, s):
    u1, u2 = x[:32], x[32:]
    return jnp.concatenate([u1 * c + u2 * s, u2 * c - u1 * s], 0)


def score_block(keys, queries, b, bias_ref, tri):
    s = dot(keys[b * 256 : (b + 1) * 256], queries, 1, 0) * SCALE
    if b == 0:
        return jnp.where(tri, s, NEG)
    return s + bias_ref[0 if b == 1 else 1]


def triangle():
    u = lax.broadcasted_iota(jnp.int32, (256, 256), 0)
    t = lax.broadcasted_iota(jnp.int32, (256, 256), 1)
    return u <= t


def attend_body(bias, q_a, q_b, kv, cos, sin, q_out, k_out, v_out, att, lse, q_turn, k_turn):
    j = pl.program_id(0)

    @pl.when(j == 0)
    def _():
        q_turn[:Q_A] = q_a[...].T
        q_turn[Q_A:] = q_b[...].T
        turned_kv = kv[...].T
        k_turn[...] = turned_kv[:KVD]
        v_out[...] = turned_kv[KVD:].astype(BF)

    c, s = cos[...], sin[...]
    head = pl.ds(pl.multiple_of(j * HEAD, HEAD), HEAD)
    kb = turned(k_turn[head, :], c, s).astype(BF)
    k_out[...] = kb
    keys = kb.T
    tri = triangle()
    for g in range(GROUP):
        rows = slice(g * HEAD, (g + 1) * HEAD)
        mine = pl.ds(pl.multiple_of((j * GROUP + g) * HEAD, HEAD), HEAD)
        qb = turned(q_turn[mine, :], c[:, :256], s[:, :256]).astype(BF)
        q_out[rows, :] = qb
        parts = [score_block(keys, qb, b, bias, tri) for b in range(4)]
        tops = [jnp.max(p, 0, keepdims=True) for p in parts]
        top = jnp.maximum(jnp.maximum(tops[0], tops[1]), jnp.maximum(tops[2], tops[3]))
        total = jnp.zeros_like(top)
        out = jnp.zeros((HEAD, 256), F32)
        for b in range(4):
            p = jnp.exp(parts[b] - top)
            total = total + jnp.sum(p, 0, keepdims=True)
            out = out + dot(v_out[head, b * 256 : (b + 1) * 256], p.astype(BF), 1, 0)
        att[rows, :] = (out / total).astype(BF)
        lse[0, g : g + 1, :] = top + jnp.log(total)
    lse[0, GROUP:, :] = jnp.zeros((8 - GROUP, 256), F32)


def attend_back_body(bias, q, k, v, d, lse, cos, sin, dq_a, dq_b, dkv, dq_turn, dkv_turn):
    j = pl.program_id(0)
    c, s = cos[...], sin[...]
    keys, values = k[...].T, v[...].T
    tri = triangle()
    dk_sum = [jnp.zeros((HEAD, 256), F32) for _ in range(4)]
    dv_sum = [jnp.zeros((HEAD, 256), F32) for _ in range(4)]
    for g in range(GROUP):
        rows = slice(g * HEAD, (g + 1) * HEAD)
        qb, db = q[rows, :], d[rows, :]
        log_total = lse[0, g : g + 1, :]
        probs, grads = [], []
        inner = jnp.zeros((1, 256), F32)
        for b in range(4):
            p = jnp.exp(score_block(keys, qb, b, bias, tri) - log_total)
            gp = dot(values[b * 256 : (b + 1) * 256], db, 1, 0)
            inner = inner + jnp.sum(p * gp, 0, keepdims=True)
            probs.append(p)
            grads.append(gp)
        dq_sum = jnp.zeros((HEAD, 256), F32)
        for b in range(4):
            ds = (probs[b] * (grads[b] - inner) * SCALE).astype(BF)
            dv_sum[b] = dv_sum[b] + dot(db, probs[b].astype(BF), 1, 1)
            dk_sum[b] = dk_sum[b] + dot(qb, ds, 1, 1)
            dq_sum = dq_sum + dot(k[:, b * 256 : (b + 1) * 256], ds, 1, 0)
        mine = pl.ds(pl.multiple_of((j * GROUP + g) * HEAD, HEAD), HEAD)
        dq_turn[mine, :] = turned_back(dq_sum, c[:, :256], s[:, :256]).astype(BF)
    dk_rows = pl.ds(pl.multiple_of(j * HEAD, HEAD), HEAD)
    dv_rows = pl.ds(pl.multiple_of((KVH + j) * HEAD, HEAD), HEAD)
    for b in range(4):
        cols = slice(b * 256, (b + 1) * 256)
        dkv_turn[dk_rows, cols] = turned_back(dk_sum[b], c[:, cols], s[:, cols]).astype(BF)
        dkv_turn[dv_rows, cols] = dv_sum[b].astype(BF)

    @pl.when(j == KVH - 1)
    def _():
        dq_a[...] = dq_turn[:Q_A].T
        dq_b[...] = dq_turn[Q_A:].T
        dkv[...] = dkv_turn[...].T


def per_head(rows, cols):
    return pl.BlockSpec((rows, cols), lambda j: (j, 0))


def whole(rows, cols):
    return pl.BlockSpec((rows, cols), lambda j: (0, 0))


LSE_SPEC = pl.BlockSpec((1, 8, 256), lambda j: (j, 0, 0))
SMEM_SPEC = pl.BlockSpec(memory_space=pltpu.SMEM)
QD, KVD = QH * HEAD, KVH * HEAD


LIGHT = pl.CostEstimate(flops=1000, transcendentals=0, bytes_accessed=1000)


def attend(bias, q_a, q_b, kv, cos, sin):
    return pl.pallas_call(
        attend_body,
        grid=(KVH,),
        in_specs=[SMEM_SPEC, whole(256, Q_A), whole(256, Q_B), whole(1024, KV), whole(32, 1024), whole(32, 1024)],
        out_specs=[
            per_head(GROUP * HEAD, 256),
            per_head(HEAD, 1024),
            whole(KVD, 1024),
            per_head(GROUP * HEAD, 256),
            LSE_SPEC,
        ],
        out_shape=[
            jax.ShapeDtypeStruct((QD, 256), BF),
            jax.ShapeDtypeStruct((KVD, 1024), BF),
            jax.ShapeDtypeStruct((KVD, 1024), BF),
            jax.ShapeDtypeStruct((QD, 256), BF),
            jax.ShapeDtypeStruct((KVH, 8, 256), F32),
        ],
        scratch_shapes=[pltpu.VMEM((QD, 256), F32), pltpu.VMEM((KVD, 1024), F32)],
        cost_estimate=LIGHT,
        name="attend",
    )(bias, q_a, q_b, kv, cos, sin)


def attend_back(bias, q, k, v, d, lse, cos, sin):
    return pl.pallas_call(
        attend_back_body,
        grid=(KVH,),
        in_specs=[
            SMEM_SPEC,
            per_head(GROUP * HEAD, 256),
            per_head(HEAD, 1024),
            per_head(HEAD, 1024),
            per_head(GROUP * HEAD, 256),
            LSE_SPEC,
            whole(32, 1024),
            whole(32, 1024),
        ],
        out_specs=[whole(256, Q_A), whole(256, Q_B), whole(1024, KV)],
        out_shape=[
            jax.ShapeDtypeStruct((256, Q_A), BF),
            jax.ShapeDtypeStruct((256, Q_B), BF),
            jax.ShapeDtypeStruct((1024, KV), BF),
        ],
        scratch_shapes=[pltpu.VMEM((QD, 256), BF), pltpu.VMEM((2 * KVD, 1024), BF)],
        cost_estimate=LIGHT,
        name="attend_back",
    )(bias, q, k, v, d, lse, cos, sin)


def ff_grads_body(tokens, grads, gate, up, act, kept, sent):
    for i, (left, right) in enumerate(((tokens, gate), (tokens, up), (grads, act))):
        turned_left = left[...].T
        for half, out in enumerate((kept, sent)):
            w = dot(turned_left, right[:, half * FF_PAD : (half + 1) * FF_PAD], 1, 0)
            out[:, i * FF_PAD : (i + 1) * FF_PAD] = w.astype(BF)


def ff_grads(tokens, grads, gate, up, act):
    width = tokens.shape[1]
    return pl.pallas_call(
        ff_grads_body,
        out_shape=[jax.ShapeDtypeStruct((width, 3 * FF_PAD), BF)] * 2,
        cost_estimate=LIGHT,
        name="ff_grads",
    )(tokens, grads, gate, up, act)


def qkv_grads_body(bias, own, every, dq_a, dq_b, dkv, kept, sent, a, b):
    own_t = own[...].T
    a[:, :Q_A] = dot(own_t, dq_a[...], 1, 0).astype(BF)
    a[:, Q_A:] = jnp.zeros((a.shape[0], HALF_W - Q_A), BF)
    b[:, :KV] = dot(every[...].T, dkv[...], 1, 0).astype(BF)
    b[:, KV:] = jnp.zeros((b.shape[0], HALF_W - KV), BF)
    b[:, KV:GAIN_AT] = dot(own_t, dq_b[...], 1, 0).astype(BF)

    @pl.when(bias[0] < -1.0)
    def _():
        kept[...] = a[...]
        sent[...] = b[...]

    @pl.when(bias[0] >= -1.0)
    def _():
        kept[...] = b[...]
        sent[...] = a[...]


def qkv_grads(bias, own, every, dq_a, dq_b, dkv):
    width = own.shape[1]
    vmem = pl.BlockSpec(memory_space=pltpu.VMEM)
    return pl.pallas_call(
        qkv_grads_body,
        in_specs=[SMEM_SPEC] + [vmem] * 5,
        out_shape=[jax.ShapeDtypeStruct((width, HALF_W), BF)] * 2,
        scratch_shapes=[pltpu.VMEM((width, HALF_W), BF)] * 2,
        cost_estimate=LIGHT,
        name="qkv_grads",
    )(bias, own, every, dq_a, dq_b, dkv)


def shards(
    inputs,
    seq_live,
    positions,
    gain_attn,
    w_query,
    w_key,
    w_value,
    w_out,
    gain_mlp,
    w_gate,
    w_up,
    w_down,
    cotangent,
):
    ctx = lax.axis_index("ctx")
    core = ctx & 1
    first = core == 0
    bias = jnp.where(jnp.stack([core == 1, ctx >= 2]), 0.0, NEG).astype(F32)
    x = inputs[0]
    rows, width = x.shape
    part = w_query.shape[0]

    gains = jnp.pad(jnp.stack([gain_attn, gain_mlp], 1), ((0, 0), (0, HALF_W - GAIN_AT - 2)))
    half_a = jnp.concatenate([w_query[:, :Q_A], jnp.zeros((part, GAIN_AT - Q_A), BF)], 1)
    half_b = jnp.concatenate([w_key, w_value, w_query[:, Q_A:]], 1)
    qkv_mine = from_fsdp(jnp.concatenate([jnp.where(first, half_a, half_b), gains], 1))
    qkv_theirs = swap_core(qkv_mine)

    upstream = cotangent[0] * seq_live.astype(F32)[:, None]
    earlier = lax.ppermute(x, "ctx", ROW_UP)
    earlier_pos = lax.ppermute(positions, "ctx", ROW_UP)
    beside = swap_core(jnp.stack([x, earlier]))
    beside_pos = swap_core(jnp.concatenate([positions, earlier_pos], 0))
    tokens = jnp.concatenate([x, beside[0], earlier, beside[1]], 0)
    grad_rows = jnp.concatenate(tp_blocks(after(upstream.astype(BF), beside)), 0)
    all_pos = jnp.concatenate([positions, beside_pos[:1], earlier_pos, beside_pos[1:]], 1)

    out_part = jnp.where(first, w_out[:, :OUT_HALF], w_out[:, OUT_HALF:])
    out_mine = from_fsdp(after(jnp.pad(out_part, ((0, 0), (0, OUT_PAD - OUT_HALF))), qkv_mine))

    def ff_half(w):
        return jnp.pad(
            jnp.where(first, w[:, :FF_HALF], w[:, FF_HALF:]), ((0, 0), (0, FF_PAD - FF_HALF))
        )

    ff_part = jnp.concatenate([ff_half(w_gate), ff_half(w_up), ff_half(w_down)], 1)
    ff_mine = from_fsdp(after(ff_part, out_mine))
    inverse = jnp.exp(jnp.arange(32, dtype=F32) * (-2.0 * math.log(ROPE_BASE) / HEAD))
    angles = inverse[:, None] * all_pos.astype(F32)
    cos, sin = jnp.cos(angles), jnp.sin(angles)
    gain_rows = qkv_mine[:, GAIN_AT : GAIN_AT + 2].astype(F32).T
    gain_one, gain_two = gain_rows[:1], gain_rows[1:]
    full_a = jnp.where(first, qkv_mine, qkv_theirs)[:, :Q_A]
    full_b = jnp.where(first, qkv_theirs, qkv_mine)[:, :GAIN_AT]
    full_kv, full_qb = full_b[:, :KV], full_b[:, KV:]
    _, _, hidden_all = rms_forward(tokens.astype(F32), gain_one)
    stream = x.astype(F32)
    inv_one, normed_one, hidden_one = rms_forward(stream, gain_one)
    q_a, q_b = dot(hidden_one, full_a, 1, 0), dot(hidden_one, full_qb, 1, 0)
    kv_lin = dot(hidden_all, full_kv, 1, 0)
    out_theirs = swap_core(after(out_mine, q_a, kv_lin))
    queries, keys, values, attended, lse = attend(bias, q_a, q_b, kv_lin, cos, sin)

    full_out = jnp.concatenate(
        [
            jnp.where(first, out_mine, out_theirs)[:, :OUT_HALF],
            jnp.where(first, out_theirs, out_mine)[:, :OUT_HALF],
        ],
        1,
    )
    mid = stream + dot(attended, full_out, 0, 0)
    inv_two, normed_two, hidden_two = rms_forward(mid, gain_two)

    ff_theirs = swap_core(after(ff_mine, attended))
    full_gate, full_up, full_down = (
        jnp.concatenate(
            [ff_mine[:, i * FF_PAD : (i + 1) * FF_PAD], ff_theirs[:, i * FF_PAD : (i + 1) * FF_PAD]],
            1,
        )
        for i in range(3)
    )

    mlp_in = jnp.concatenate(tp_blocks(hidden_two), 0)
    gate_pre = dot(mlp_in, full_gate, 1, 0)
    up_pre = dot(mlp_in, full_up, 1, 0)
    sg = jax.nn.sigmoid(gate_pre)
    grad_act = dot(grad_rows, full_down, 1, 0)
    up_back = (grad_act * gate_pre * sg).astype(BF)
    gate_back = (grad_act * up_pre * sg * (1.0 + gate_pre * (1.0 - sg))).astype(BF)
    activated = (gate_pre * sg * up_pre).astype(BF)
    partial_in = dot(gate_back, full_gate, 1, 1) + dot(up_back, full_up, 1, 1)
    partial_in = partial_in.reshape(4, rows, width)
    sent_in = [partial_in[i].astype(BF) for i in (1, 2, 3)]

    mlp_in, gate_back, up_back, activated, *sent_in = lax.optimization_barrier(
        (mlp_in, gate_back, up_back, activated, *sent_in)
    )
    ff_kept, ff_sent = ff_grads(mlp_in, grad_rows, gate_back, up_back, activated)
    ff_pair = (ff_kept.astype(F32) + swap_core(ff_sent).astype(F32)).astype(BF)
    ff_arrived = to_fsdp(ff_pair)
    grad_hidden_two = tp_sum(after(partial_in[0], ff_kept), *sent_in)

    partial_out = dot(after(activated, grad_hidden_two), full_down, 1, 1).reshape(4, rows, width)
    sent_out = [partial_out[i].astype(BF) for i in (1, 2, 3)]

    back_two, dgain_two = rms_backward(grad_hidden_two, inv_two, normed_two, gain_two)
    grad_mid = upstream + back_two
    grad_mid_b = grad_mid.astype(BF)
    grad_attended = dot(full_out, grad_mid_b, 1, 1).astype(BF)
    dw_out = dot(attended, grad_mid_b, 1, 0).astype(BF)
    pad_out = ((0, 0), (0, OUT_PAD - OUT_HALF))
    out_l = jnp.pad(dw_out[:, :OUT_HALF], pad_out)
    out_r = jnp.pad(dw_out[:, OUT_HALF:], pad_out)
    out_kept, out_sent = jnp.where(first, out_l, out_r), jnp.where(first, out_r, out_l)
    out_pair = (out_kept.astype(F32) + swap_core(out_sent).astype(F32)).astype(BF)
    grad_attended, *sent_out = lax.optimization_barrier((grad_attended, *sent_out, out_pair))[:4]
    dq_a, dq_b, dkv = attend_back(bias, queries, keys, values, grad_attended, lse, cos, sin)
    qkv_kept, qkv_sent = qkv_grads(bias, hidden_one, hidden_all, dq_a, dq_b, dkv)
    layer_out = mid + tp_sum(after(partial_out[0], qkv_kept), *sent_out)
    qkv_sent = after(qkv_sent, layer_out)

    ff_sum = summed(after(ff_arrived, dkv))
    out_arrived = to_fsdp(after(out_pair, ff_arrived))

    from_beside = swap_core(jnp.concatenate([dkv[256:512], dkv[768:]], 0))
    own_pair = dkv[:256].astype(F32) + from_beside[:256].astype(F32)
    earlier_pair = dkv[512:768].astype(F32) + from_beside[256:].astype(F32)
    from_later = lax.ppermute(earlier_pair.astype(BF), "ctx", ROW_DOWN)
    own_kv = (own_pair + from_later.astype(F32)).astype(BF)
    grad_hidden_one = (
        dot(dq_a, full_a, 1, 1) + dot(dq_b, full_qb, 1, 1) + dot(own_kv, full_kv, 1, 1)
    )
    back_one, dgain_one = rms_backward(grad_hidden_one, inv_one, normed_one, gain_one)
    grad_input = grad_mid + back_one

    gain_columns = jnp.pad(
        jnp.stack([dgain_one, dgain_two], 1), ((0, 0), (GAIN_AT, HALF_W - GAIN_AT - 2))
    )
    qkv_pair = qkv_kept.astype(F32) + swap_core(qkv_sent).astype(F32)
    qkv_pair = (qkv_pair + gain_columns).astype(BF)
    qkv_arrived = to_fsdp(after(qkv_pair, out_arrived))
    out_sum = summed(after(out_arrived, qkv_pair))

    def both_rows(v):
        return v.astype(F32) + lax.ppermute(v, "ctx", ROW_SWAP).astype(F32)

    def all_tp(v):
        for pairs in ([(0, 1), (1, 0), (2, 3), (3, 2)], [(0, 3), (3, 0), (1, 2), (2, 1)]):
            v = (v.astype(F32) + lax.ppermute(v, "tp", pairs).astype(F32)).astype(BF)
        return v

    out_own = both_rows(all_tp(out_sum))
    out_other = swap_core(out_own)
    ff_own = both_rows(ff_sum)
    ff_other = swap_core(ff_own)
    qkv_own = both_rows(all_tp(summed(after(qkv_arrived, out_other, ff_other))))
    qkv_other = swap_core(qkv_own)
    ff_lo, ff_hi = jnp.where(first, ff_own, ff_other), jnp.where(first, ff_other, ff_own)
    dw_gate, dw_up, dw_down = (
        jnp.concatenate([v[:, i * FF_PAD : i * FF_PAD + FF_HALF] for v in (ff_lo, ff_hi)], 1)
        for i in range(3)
    )
    out_lo, out_hi = jnp.where(first, out_own, out_other), jnp.where(first, out_other, out_own)
    dw_out = jnp.concatenate([out_lo[:, :OUT_HALF], out_hi[:, :OUT_HALF]], 1)
    got_a, got_b = jnp.where(first, qkv_own, qkv_other), jnp.where(first, qkv_other, qkv_own)
    return (
        layer_out[None],
        grad_input[None],
        got_a[:, GAIN_AT] + got_b[:, GAIN_AT],
        jnp.concatenate([got_a[:, :Q_A], got_b[:, KV:GAIN_AT]], 1),
        got_b[:, :KVD],
        got_b[:, KVD:KV],
        dw_out,
        got_a[:, GAIN_AT + 1] + got_b[:, GAIN_AT + 1],
        dw_gate,
        dw_up,
        dw_down,
    )


def solution(mesh):
    seqs, tokens = P(("fsdp", "tp"), "ctx", None), P(("fsdp", "tp"), "ctx")
    row, both = P("fsdp", None), P("fsdp", "tp")
    return jax.shard_map(
        shards,
        mesh=mesh,
        in_specs=(seqs, P(("fsdp", "tp")), tokens, P("fsdp"), row, row, row, row, P("fsdp"), both, both, both, seqs),
        out_specs=(seqs, seqs, P("fsdp"), row, row, row, row, P("fsdp"), both, both, both),
        check_vma=False,
    )
```

```python
import math

import jax
import jax.numpy as jnp
from jax import lax
from jax.experimental import pallas as pl
from jax.experimental.pallas import tpu as pltpu
from jax.sharding import PartitionSpec as P

QH = 15
KVH = 5
HEAD = 64
GROUP = QH // KVH
EPSILON = 1e-05
ROPE_BASE = 100000.0
SCALE = 1.0 / math.sqrt(HEAD)
NEG = -1e30
BF = jnp.bfloat16
F32 = jnp.float32

Q_A = 768
Q_B = 192
KV = 640
GAIN_AT = 832
HALF_W = 896
FF_HALF = 320
FF_PAD = 384
OUT_HALF = 480
OUT_PAD = 512

CORE_SWAP = [(i, i ^ 1) for i in range(4)]
ROW_SWAP = [(i, i ^ 2) for i in range(4)]
ROW_UP = [(0, 2), (1, 3)]
ROW_DOWN = [(2, 0), (3, 1)]


def dot(a, b, ca, cb):
    return lax.dot_general(a, b, (((ca,), (cb,)), ((), ())), preferred_element_type=F32)


def after(value, *others):
    return lax.optimization_barrier((value, *others))[0]


def from_fsdp(shard):
    copies = jnp.broadcast_to(shard, (lax.axis_size("fsdp"), *shard.shape))
    out = lax.all_to_all(copies, "fsdp", split_axis=0, concat_axis=0, tiled=True)
    return out.reshape(-1, shard.shape[1])


def to_fsdp(full):
    n = lax.axis_size("fsdp")
    tiles = full.reshape(n, full.shape[0] // n, full.shape[1])
    return lax.all_to_all(tiles, "fsdp", split_axis=0, concat_axis=0, tiled=True)


def summed(arrived):
    return arrived.astype(F32).sum(axis=0).astype(BF)


def shift(x, by):
    return lax.ppermute(x, "tp", [(i, (i + by) % 4) for i in range(4)])


def tp_beside(x):
    return shift(x, 1), shift(x, 3)


def tp_far(left, right):
    half = left.shape[0] // 2
    return shift(left[:half], 1), shift(right[half:], 3)


def tp_sum(own, left, right, far):
    a, b, c = shift(left, 3), shift(right, 1), shift(far, 2)
    return own + a.astype(F32) + b.astype(F32) + c.astype(F32)


def swap_core(x):
    return lax.ppermute(x, "ctx", CORE_SWAP)


def rms_forward(stream, gain_row):
    scale_inv = lax.rsqrt(jnp.mean(stream * stream, -1, keepdims=True) + EPSILON)
    normed = stream * scale_inv
    return scale_inv, normed, (normed * gain_row).astype(BF)


def rms_backward(upstream, scale_inv, normed, gain_row):
    scaled = upstream * gain_row
    inner_mean = jnp.mean(scaled * normed, -1, keepdims=True)
    return scale_inv * (scaled - normed * inner_mean), jnp.sum(upstream * normed, 0)


def turned(x, c, s):
    u1, u2 = x[:32], x[32:]
    return jnp.concatenate([u1 * c - u2 * s, u2 * c + u1 * s], 0)


def turned_back(x, c, s):
    u1, u2 = x[:32], x[32:]
    return jnp.concatenate([u1 * c + u2 * s, u2 * c - u1 * s], 0)


def score_block(keys, queries, b, bias_ref, tri):
    s = dot(keys[b * 256 : (b + 1) * 256], queries, 1, 0) * SCALE
    if b == 0:
        return jnp.where(tri, s, NEG)
    return s + bias_ref[0 if b == 1 else 1]


def triangle():
    u = lax.broadcasted_iota(jnp.int32, (256, 256), 0)
    t = lax.broadcasted_iota(jnp.int32, (256, 256), 1)
    return u <= t


def attend_body(bias, q_a, q_b, kv, cos, sin, q_out, k_out, v_out, att, lse, q_turn, k_turn):
    j = pl.program_id(0)

    @pl.when(j == 0)
    def _():
        q_turn[:Q_A] = q_a[...].T
        q_turn[Q_A:] = q_b[...].T
        turned_kv = kv[...].T
        k_turn[...] = turned_kv[:KVD]
        v_out[...] = turned_kv[KVD:].astype(BF)

    c, s = cos[...], sin[...]
    head = pl.ds(pl.multiple_of(j * HEAD, HEAD), HEAD)
    kb = turned(k_turn[head, :], c, s).astype(BF)
    k_out[...] = kb
    keys = kb.T
    tri = triangle()
    for g in range(GROUP):
        rows = slice(g * HEAD, (g + 1) * HEAD)
        mine = pl.ds(pl.multiple_of((j * GROUP + g) * HEAD, HEAD), HEAD)
        qb = turned(q_turn[mine, :], c[:, :256], s[:, :256]).astype(BF)
        q_out[rows, :] = qb
        parts = [score_block(keys, qb, b, bias, tri) for b in range(4)]
        tops = [jnp.max(p, 0, keepdims=True) for p in parts]
        top = jnp.maximum(jnp.maximum(tops[0], tops[1]), jnp.maximum(tops[2], tops[3]))
        total = jnp.zeros_like(top)
        out = jnp.zeros((HEAD, 256), F32)
        for b in range(4):
            p = jnp.exp(parts[b] - top)
            total = total + jnp.sum(p, 0, keepdims=True)
            out = out + dot(v_out[head, b * 256 : (b + 1) * 256], p.astype(BF), 1, 0)
        att[rows, :] = (out / total).astype(BF)
        lse[0, g : g + 1, :] = top + jnp.log(total)
    lse[0, GROUP:, :] = jnp.zeros((8 - GROUP, 256), F32)


def attend_back_body(bias, q, k, v, d, lse, cos, sin, dq_a, dq_b, dkv, dq_turn, dkv_turn):
    j = pl.program_id(0)
    c, s = cos[...], sin[...]
    keys, values = k[...].T, v[...].T
    tri = triangle()
    dk_sum = [jnp.zeros((HEAD, 256), F32) for _ in range(4)]
    dv_sum = [jnp.zeros((HEAD, 256), F32) for _ in range(4)]
    for g in range(GROUP):
        rows = slice(g * HEAD, (g + 1) * HEAD)
        qb, db = q[rows, :], d[rows, :]
        log_total = lse[0, g : g + 1, :]
        probs, grads = [], []
        inner = jnp.zeros((1, 256), F32)
        for b in range(4):
            p = jnp.exp(score_block(keys, qb, b, bias, tri) - log_total)
            gp = dot(values[b * 256 : (b + 1) * 256], db, 1, 0)
            inner = inner + jnp.sum(p * gp, 0, keepdims=True)
            probs.append(p)
            grads.append(gp)
        dq_sum = jnp.zeros((HEAD, 256), F32)
        for b in range(4):
            ds = (probs[b] * (grads[b] - inner) * SCALE).astype(BF)
            dv_sum[b] = dv_sum[b] + dot(db, probs[b].astype(BF), 1, 1)
            dk_sum[b] = dk_sum[b] + dot(qb, ds, 1, 1)
            dq_sum = dq_sum + dot(k[:, b * 256 : (b + 1) * 256], ds, 1, 0)
        mine = pl.ds(pl.multiple_of((j * GROUP + g) * HEAD, HEAD), HEAD)
        dq_turn[mine, :] = turned_back(dq_sum, c[:, :256], s[:, :256]).astype(BF)
    dk_rows = pl.ds(pl.multiple_of(j * HEAD, HEAD), HEAD)
    dv_rows = pl.ds(pl.multiple_of((KVH + j) * HEAD, HEAD), HEAD)
    for b in range(4):
        cols = slice(b * 256, (b + 1) * 256)
        dkv_turn[dk_rows, cols] = turned_back(dk_sum[b], c[:, cols], s[:, cols]).astype(BF)
        dkv_turn[dv_rows, cols] = dv_sum[b].astype(BF)

    @pl.when(j == KVH - 1)
    def _():
        dq_a[...] = dq_turn[:Q_A].T
        dq_b[...] = dq_turn[Q_A:].T
        dkv[...] = dkv_turn[...].T


def per_head(rows, cols):
    return pl.BlockSpec((rows, cols), lambda j: (j, 0))


def whole(rows, cols):
    return pl.BlockSpec((rows, cols), lambda j: (0, 0))


LSE_SPEC = pl.BlockSpec((1, 8, 256), lambda j: (j, 0, 0))
SMEM_SPEC = pl.BlockSpec(memory_space=pltpu.SMEM)
QD, KVD = QH * HEAD, KVH * HEAD


LIGHT = pl.CostEstimate(flops=1000, transcendentals=0, bytes_accessed=1000)


def attend(bias, q_a, q_b, kv, cos, sin):
    return pl.pallas_call(
        attend_body,
        grid=(KVH,),
        in_specs=[SMEM_SPEC, whole(256, Q_A), whole(256, Q_B), whole(1024, KV), whole(32, 1024), whole(32, 1024)],
        out_specs=[
            per_head(GROUP * HEAD, 256),
            per_head(HEAD, 1024),
            whole(KVD, 1024),
            per_head(GROUP * HEAD, 256),
            LSE_SPEC,
        ],
        out_shape=[
            jax.ShapeDtypeStruct((QD, 256), BF),
            jax.ShapeDtypeStruct((KVD, 1024), BF),
            jax.ShapeDtypeStruct((KVD, 1024), BF),
            jax.ShapeDtypeStruct((QD, 256), BF),
            jax.ShapeDtypeStruct((KVH, 8, 256), F32),
        ],
        scratch_shapes=[pltpu.VMEM((QD, 256), F32), pltpu.VMEM((KVD, 1024), F32)],
        cost_estimate=LIGHT,
        name="attend",
    )(bias, q_a, q_b, kv, cos, sin)


def attend_back(bias, q, k, v, d, lse, cos, sin):
    return pl.pallas_call(
        attend_back_body,
        grid=(KVH,),
        in_specs=[
            SMEM_SPEC,
            per_head(GROUP * HEAD, 256),
            per_head(HEAD, 1024),
            per_head(HEAD, 1024),
            per_head(GROUP * HEAD, 256),
            LSE_SPEC,
            whole(32, 1024),
            whole(32, 1024),
        ],
        out_specs=[whole(256, Q_A), whole(256, Q_B), whole(1024, KV)],
        out_shape=[
            jax.ShapeDtypeStruct((256, Q_A), BF),
            jax.ShapeDtypeStruct((256, Q_B), BF),
            jax.ShapeDtypeStruct((1024, KV), BF),
        ],
        scratch_shapes=[pltpu.VMEM((QD, 256), BF), pltpu.VMEM((2 * KVD, 1024), BF)],
        cost_estimate=LIGHT,
        name="attend_back",
    )(bias, q, k, v, d, lse, cos, sin)


def ff_grads_body(tokens, grads, gate, up, act, kept, sent):
    for i, (left, right) in enumerate(((tokens, gate), (tokens, up), (grads, act))):
        turned_left = left[...].T
        for half, out in enumerate((kept, sent)):
            w = dot(turned_left, right[:, half * FF_PAD : (half + 1) * FF_PAD], 1, 0)
            out[:, i * FF_PAD : (i + 1) * FF_PAD] = w.astype(BF)


def ff_grads(tokens, grads, gate, up, act):
    width = tokens.shape[1]
    return pl.pallas_call(
        ff_grads_body,
        out_shape=[jax.ShapeDtypeStruct((width, 3 * FF_PAD), BF)] * 2,
        cost_estimate=LIGHT,
        name="ff_grads",
    )(tokens, grads, gate, up, act)


def qkv_grads_body(bias, own, every, dq_a, dq_b, dkv, kept, sent, a, b):
    own_t = own[...].T
    a[:, :Q_A] = dot(own_t, dq_a[...], 1, 0).astype(BF)
    a[:, Q_A:] = jnp.zeros((a.shape[0], HALF_W - Q_A), BF)
    b[:, :KV] = dot(every[...].T, dkv[...], 1, 0).astype(BF)
    b[:, KV:] = jnp.zeros((b.shape[0], HALF_W - KV), BF)
    b[:, KV:GAIN_AT] = dot(own_t, dq_b[...], 1, 0).astype(BF)

    @pl.when(bias[0] < -1.0)
    def _():
        kept[...] = a[...]
        sent[...] = b[...]

    @pl.when(bias[0] >= -1.0)
    def _():
        kept[...] = b[...]
        sent[...] = a[...]


def qkv_grads(bias, own, every, dq_a, dq_b, dkv):
    width = own.shape[1]
    vmem = pl.BlockSpec(memory_space=pltpu.VMEM)
    return pl.pallas_call(
        qkv_grads_body,
        in_specs=[SMEM_SPEC] + [vmem] * 5,
        out_shape=[jax.ShapeDtypeStruct((width, HALF_W), BF)] * 2,
        scratch_shapes=[pltpu.VMEM((width, HALF_W), BF)] * 2,
        cost_estimate=LIGHT,
        name="qkv_grads",
    )(bias, own, every, dq_a, dq_b, dkv)


def shards(
    inputs,
    seq_live,
    positions,
    gain_attn,
    w_query,
    w_key,
    w_value,
    w_out,
    gain_mlp,
    w_gate,
    w_up,
    w_down,
    cotangent,
):
    ctx = lax.axis_index("ctx")
    core = ctx & 1
    first = core == 0
    bias = jnp.where(jnp.stack([core == 1, ctx >= 2]), 0.0, NEG).astype(F32)
    x = inputs[0]
    rows, width = x.shape
    part = w_query.shape[0]

    gains = jnp.pad(jnp.stack([gain_attn, gain_mlp], 1), ((0, 0), (0, HALF_W - GAIN_AT - 2)))
    half_a = jnp.concatenate([w_query[:, :Q_A], jnp.zeros((part, GAIN_AT - Q_A), BF)], 1)
    half_b = jnp.concatenate([w_key, w_value, w_query[:, Q_A:]], 1)
    qkv_mine = from_fsdp(jnp.concatenate([jnp.where(first, half_a, half_b), gains], 1))
    qkv_theirs = swap_core(qkv_mine)

    upstream = cotangent[0] * seq_live.astype(F32)[:, None]
    earlier = lax.ppermute(x, "ctx", ROW_UP)
    earlier_pos = lax.ppermute(positions, "ctx", ROW_UP)
    beside = swap_core(jnp.stack([x, earlier]))
    beside_pos = swap_core(jnp.concatenate([positions, earlier_pos], 0))
    tokens = jnp.concatenate([x, beside[0], earlier, beside[1]], 0)
    upstream_b = upstream.astype(BF)
    grads_left, grads_right = tp_beside(after(upstream_b, beside))
    all_pos = jnp.concatenate([positions, beside_pos[:1], earlier_pos, beside_pos[1:]], 1)

    out_part = jnp.where(first, w_out[:, :OUT_HALF], w_out[:, OUT_HALF:])
    out_mine = from_fsdp(after(jnp.pad(out_part, ((0, 0), (0, OUT_PAD - OUT_HALF))), qkv_mine))

    def ff_half(w):
        return jnp.pad(
            jnp.where(first, w[:, :FF_HALF], w[:, FF_HALF:]), ((0, 0), (0, FF_PAD - FF_HALF))
        )

    ff_part = jnp.concatenate([ff_half(w_gate), ff_half(w_up), ff_half(w_down)], 1)

    inverse = jnp.exp(jnp.arange(32, dtype=F32) * (-2.0 * math.log(ROPE_BASE) / HEAD))
    angles = inverse[:, None] * all_pos.astype(F32)
    cos, sin = jnp.cos(angles), jnp.sin(angles)
    gain_rows = qkv_mine[:, GAIN_AT : GAIN_AT + 2].astype(F32).T
    gain_one, gain_two = gain_rows[:1], gain_rows[1:]
    qkv_theirs, grads_left, grads_right, cos, sin = lax.optimization_barrier(
        (qkv_theirs, grads_left, grads_right, cos, sin)
    )
    grads_far = tp_far(grads_left, grads_right)
    full_a = jnp.where(first, qkv_mine, qkv_theirs)[:, :Q_A]
    full_b = jnp.where(first, qkv_theirs, qkv_mine)[:, :GAIN_AT]
    full_kv, full_qb = full_b[:, :KV], full_b[:, KV:]
    _, _, hidden_all = rms_forward(tokens.astype(F32), gain_one)
    stream = x.astype(F32)
    inv_one, normed_one, hidden_one = rms_forward(stream, gain_one)
    q_a, q_b = dot(hidden_one, full_a, 1, 0), dot(hidden_one, full_qb, 1, 0)
    kv_lin = dot(hidden_all, full_kv, 1, 0)
    out_mine = after(out_mine, q_a, kv_lin)
    out_theirs = swap_core(out_mine)
    ff_mine = from_fsdp(after(ff_part, out_mine))
    queries, keys, values, attended, lse = attend(bias, q_a, q_b, kv_lin, cos, sin)
    attended, *grads_far = lax.optimization_barrier((attended, *grads_far))
    grad_rows = jnp.concatenate([upstream_b, grads_left, grads_right, *grads_far], 0)

    full_out = jnp.concatenate(
        [
            jnp.where(first, out_mine, out_theirs)[:, :OUT_HALF],
            jnp.where(first, out_theirs, out_mine)[:, :OUT_HALF],
        ],
        1,
    )
    mid = stream + dot(attended, full_out, 0, 0)
    inv_two, normed_two, hidden_two = rms_forward(mid, gain_two)

    ff_theirs = swap_core(after(ff_mine, attended))
    full_gate, full_up, full_down = (
        jnp.concatenate(
            [ff_mine[:, i * FF_PAD : (i + 1) * FF_PAD], ff_theirs[:, i * FF_PAD : (i + 1) * FF_PAD]],
            1,
        )
        for i in range(3)
    )

    tokens_left, tokens_right = tp_beside(hidden_two)
    tokens_far = tp_far(tokens_left, tokens_right)
    mlp_in = jnp.concatenate([hidden_two, tokens_left, tokens_right, *tokens_far], 0)
    gate_pre = dot(mlp_in, full_gate, 1, 0)
    up_pre = dot(mlp_in, full_up, 1, 0)
    sg = jax.nn.sigmoid(gate_pre)
    grad_act = dot(grad_rows, full_down, 1, 0)
    up_back = (grad_act * gate_pre * sg).astype(BF)
    gate_back = (grad_act * up_pre * sg * (1.0 + gate_pre * (1.0 - sg))).astype(BF)
    activated = (gate_pre * sg * up_pre).astype(BF)
    partial_in = dot(gate_back, full_gate, 1, 1) + dot(up_back, full_up, 1, 1)
    partial_in = partial_in.reshape(4, rows, width)
    sent_in = [partial_in[i].astype(BF) for i in (1, 2, 3)]

    mlp_in, gate_back, up_back, activated, *sent_in = lax.optimization_barrier(
        (mlp_in, gate_back, up_back, activated, *sent_in)
    )
    ff_kept, ff_sent = ff_grads(mlp_in, grad_rows, gate_back, up_back, activated)
    ff_pair = ff_kept.astype(F32) + swap_core(ff_sent).astype(F32)
    grad_hidden_two = tp_sum(after(partial_in[0], ff_kept), *sent_in)

    partial_out = dot(after(activated, grad_hidden_two), full_down, 1, 1).reshape(4, rows, width)
    sent_out = [partial_out[i].astype(BF) for i in (1, 2, 3)]

    back_two, dgain_two = rms_backward(grad_hidden_two, inv_two, normed_two, gain_two)
    grad_mid = upstream + back_two
    grad_mid_b = grad_mid.astype(BF)
    grad_attended = dot(full_out, grad_mid_b, 1, 1).astype(BF)
    dw_out = dot(attended, grad_mid_b, 1, 0).astype(BF)
    pad_out = ((0, 0), (0, OUT_PAD - OUT_HALF))
    out_l = jnp.pad(dw_out[:, :OUT_HALF], pad_out)
    out_r = jnp.pad(dw_out[:, OUT_HALF:], pad_out)
    out_kept, out_sent = jnp.where(first, out_l, out_r), jnp.where(first, out_r, out_l)
    gain_column = jnp.pad(dgain_two[:, None], ((0, 0), (OUT_HALF, OUT_PAD - OUT_HALF - 1)))
    out_pair = out_kept.astype(F32) + swap_core(out_sent).astype(F32) + gain_column
    early_pair = jnp.concatenate([ff_pair.astype(BF), out_pair.astype(BF)], 1)
    early_arrived = to_fsdp(early_pair)
    grad_attended, *sent_out = lax.optimization_barrier((grad_attended, *sent_out, early_pair))[:4]
    dq_a, dq_b, dkv = attend_back(bias, queries, keys, values, grad_attended, lse, cos, sin)
    qkv_kept, qkv_sent = qkv_grads(bias, hidden_one, hidden_all, dq_a, dq_b, dkv)
    layer_out = mid + tp_sum(after(partial_out[0], qkv_kept), *sent_out)
    qkv_sent = after(qkv_sent, layer_out)

    from_beside = swap_core(jnp.concatenate([dkv[256:512], dkv[768:]], 0))
    own_pair = dkv[:256].astype(F32) + from_beside[:256].astype(F32)
    earlier_pair = dkv[512:768].astype(F32) + from_beside[256:].astype(F32)
    from_later = lax.ppermute(earlier_pair.astype(BF), "ctx", ROW_DOWN)
    own_kv = (own_pair + from_later.astype(F32)).astype(BF)
    grad_hidden_one = (
        dot(dq_a, full_a, 1, 1) + dot(dq_b, full_qb, 1, 1) + dot(own_kv, full_kv, 1, 1)
    )
    back_one, _ = rms_backward(grad_hidden_one, inv_one, normed_one, gain_one)
    grad_input = grad_mid + back_one

    qkv_pair = (qkv_kept.astype(F32) + swap_core(qkv_sent).astype(F32)).astype(BF)
    qkv_arrived = to_fsdp(after(qkv_pair, early_arrived))
    early_sum = summed(after(early_arrived, qkv_pair))

    def both_rows(v):
        return v.astype(F32) + lax.ppermute(v, "ctx", ROW_SWAP).astype(F32)

    def all_tp(v):
        for pairs in ([(0, 1), (1, 0), (2, 3), (3, 2)], [(0, 3), (3, 0), (1, 2), (2, 1)]):
            v = (v.astype(F32) + lax.ppermute(v, "tp", pairs).astype(F32)).astype(BF)
        return v

    ff_w = 3 * FF_PAD
    ff_own = both_rows(early_sum[:, :ff_w])
    ff_other = swap_core(ff_own)
    out_tp = all_tp(early_sum[:, ff_w:])
    qkv_tp = all_tp(summed(after(qkv_arrived, ff_other, out_tp)))
    qkv_own = both_rows(jnp.concatenate([qkv_tp, out_tp], 1))
    qkv_other = swap_core(qkv_own)
    ff_lo, ff_hi = jnp.where(first, ff_own, ff_other), jnp.where(first, ff_other, ff_own)
    dw_gate, dw_up, dw_down = (
        jnp.concatenate([v[:, i * FF_PAD : i * FF_PAD + FF_HALF] for v in (ff_lo, ff_hi)], 1)
        for i in range(3)
    )
    got_a, got_b = jnp.where(first, qkv_own, qkv_other), jnp.where(first, qkv_other, qkv_own)
    out_lo, out_hi = got_a[:, HALF_W:], got_b[:, HALF_W:]
    dw_out = jnp.concatenate([out_lo[:, :OUT_HALF], out_hi[:, :OUT_HALF]], 1)
    dgain_one = (
        jnp.sum(got_a[:, :Q_A] * w_query[:, :Q_A].astype(F32), 1)
        + jnp.sum(got_b[:, :GAIN_AT] * half_b.astype(F32), 1)
    ) / gain_attn.astype(F32)
    return (
        layer_out[None],
        grad_input[None],
        dgain_one,
        jnp.concatenate([got_a[:, :Q_A], got_b[:, KV:GAIN_AT]], 1),
        got_b[:, :KVD],
        got_b[:, KVD:KV],
        dw_out,
        out_lo[:, OUT_HALF] + out_hi[:, OUT_HALF],
        dw_gate,
        dw_up,
        dw_down,
    )


def solution(mesh):
    seqs, tokens = P(("fsdp", "tp"), "ctx", None), P(("fsdp", "tp"), "ctx")
    row, both = P("fsdp", None), P("fsdp", "tp")
    return jax.shard_map(
        shards,
        mesh=mesh,
        in_specs=(seqs, P(("fsdp", "tp")), tokens, P("fsdp"), row, row, row, row, P("fsdp"), both, both, both, seqs),
        out_specs=(seqs, seqs, P("fsdp"), row, row, row, row, P("fsdp"), both, both, both),
        check_vma=False,
    )
```
